32 devices in a mesh: owner: 32 (over z, y, x, core).
Axes of the slice: x: 2, y: 2, z: 4, core: 2. Of those that a mesh axis runs over, the one named last changes fastest.
Arguments:
- frontier: bfloat16 [512, 1326], P('owner'), may hold values from 0.019897461 to 1
- policy_table: bfloat16 [2048, 1326], replicated, may hold values from 0.019897461 to 1
- first_counts: int32 [512], P('owner'), may hold values from 1 to 64
- policy_index: int32 [3, 16384], P(None, 'owner'), may hold values from 0 to 2047
- owner_index: int32 [3, 16384], P(None, 'owner'), may hold values from 0 to 31
- next_counts: int32 [2, 16384], P(None, 'owner'), may hold values from 0 to 64, as said below
- value_in: bfloat16 [1326, 1536], replicated, may hold values from -0.15625 to 0.15625
- value_out: bfloat16 [1536, 1326], replicated, may hold values from -0.15625 to 0.15625
Outputs:
- leaf_values: bfloat16 [3, 16384, 1326], P(None, 'owner')
The draws below stay inside these ranges and needn't reach their ends.
Inputs may be any that keep to these rules, and one draw needn't show every extreme that they name: `next_counts`: 0 marks a belief that is not expanded.
All inputs are finite; a program needn't handle non-finite values.
Results may differ from the reference program's by a relative error of at most 0.0067.
Values may be sent and summed in bfloat16 or wider, within the bound.
A program may use at most 128 MiB of HBM per device.

```python
import math
import jax
import jax.numpy as jnp
from jax import lax

HANDS = 1326
HIDDEN_UNITS = 1536
POLICY = 2048
LEVELS = 3
MAX_CHILDREN = 64
FRONT_DEV = 16
SLOTS = 512
RECV_DEV = 512
NODE_DEV = 384
FRONTIER = 512
ALL_SLOTS = 16384
N_OWNER = 32


def owner_table(key):
    owner_key = jax.random.fold_in(key, 101)
    return jax.random.randint(owner_key, (LEVELS, SLOTS * N_OWNER), 0, N_OWNER).astype(jnp.int32)


def draw_owner_index(key, part):
    return owner_table(key)


def draw_next_counts(key, part):
    owners = owner_table(key)[:LEVELS - 1]
    grow_key = jax.random.fold_in(key, 11)
    pick_key = jax.random.fold_in(key, 23)
    rate_key = jax.random.fold_in(key, 37)
    shape_all = (LEVELS - 1, SLOTS * N_OWNER)
    exponent = jax.random.randint(rate_key, (LEVELS - 1, N_OWNER), 0, 5).astype(jnp.int32)
    divisor_table = jnp.left_shift(jnp.full((LEVELS - 1, N_OWNER), 4, jnp.int32), exponent)
    divisor = jnp.take_along_axis(divisor_table, owners, axis=1)
    grown = jax.random.randint(grow_key, shape_all, 1, MAX_CHILDREN + 1).astype(jnp.int32)
    picked = jax.random.randint(pick_key, shape_all, 0, 1 << 20).astype(jnp.int32)
    return jnp.where(picked % divisor == 0, grown, 0).astype(jnp.int32)


def plant(result, own_key, low, largest):
    shape = result.shape
    spot = [jax.random.randint(jax.random.fold_in(own_key, axis), (), 0, shape[axis]) for axis in range(len(shape))]
    result = result.at[tuple(spot)].set(low)
    longest = shape.index(max(shape))
    spot[longest] = (spot[longest] + 1) % shape[longest]
    return result.at[tuple(spot)].set(largest)


def block_scale(rng, extent, pieces, least, high):
    def one(position, parts):
        steps = jax.random.uniform(jax.random.fold_in(jax.random.fold_in(rng, 6), position), (parts,), jnp.float32, least / len(pieces), high / len(pieces))
        return jnp.repeat(jnp.exp(steps), extent[position] // parts).reshape((-1,) + (1,) * (len(extent) - position - 1))

    level = one(*pieces[0])
    for cut in pieces[1:]:
        level = level * one(*cut)
    return level


def scatter_about(own_key, extent, spread, bound, held_as=jnp.bfloat16):
    result = spread * jax.random.normal(own_key, extent, jnp.float32)
    return jnp.clip(result, min=-bound, max=bound).astype(held_as)


def setup_inputs(seed: int = 0) -> dict:
    streams_of = jax.random.split(jax.random.key(seed), 9)
    return {
        "frontier": jnp.clip(jnp.exp(math.log(1.0) - 3.9171631 * jax.random.uniform(streams_of[0], (FRONTIER, HANDS), jnp.float32) ** block_scale(streams_of[0], (FRONTIER, HANDS), ((0, 32),), -0.2, 0.2)), 0.019897461, 1.0).astype(jnp.bfloat16),
        "policy_table": jnp.clip(jnp.exp(jax.random.uniform(streams_of[1], (POLICY, HANDS), jnp.float32, math.log(0.019897461), math.log(1.0))), 0.019897461, 1.0).astype(jnp.bfloat16),
        "first_counts": plant(jax.random.randint(streams_of[2], (FRONTIER,), 1, MAX_CHILDREN + 1), jax.random.fold_in(streams_of[2], 1), 1, MAX_CHILDREN).astype(jnp.int32),
        "policy_index": plant(jax.random.randint(streams_of[3], (LEVELS, ALL_SLOTS), 0, POLICY), jax.random.fold_in(streams_of[3], 1), 0, POLICY - 1).astype(jnp.int32),
        "owner_index": draw_owner_index(jax.random.fold_in(streams_of[8], 71), 0),
        "next_counts": draw_next_counts(jax.random.fold_in(streams_of[8], 71), 0),
        "value_in": scatter_about(streams_of[6], (HANDS, HIDDEN_UNITS), HANDS ** -0.5, 0.15625),
        "value_out": scatter_about(streams_of[7], (HIDDEN_UNITS, HANDS), HIDDEN_UNITS ** -0.5, 0.15625),
    }


def count_slots(counts, slots):
    count_ends = jnp.cumsum(counts).astype(jnp.int32)
    child_total = jnp.minimum(count_ends[-1], slots).astype(jnp.int32)
    slot_index = jnp.arange(slots, dtype=jnp.int32)
    segment = jnp.sum((count_ends[None, :] <= slot_index[:, None]).astype(jnp.int32), axis=1).astype(jnp.int32)
    segment = jnp.minimum(segment, counts.shape[0] - 1).astype(jnp.int32)
    return child_total, slot_index, segment


def form_children(parent_rows, policy_rows, kept_mask):
    children = parent_rows.astype(jnp.float32) * policy_rows.astype(jnp.float32)
    child_mass = jnp.sum(children, axis=1)
    child_mass = jnp.where(kept_mask, child_mass, jnp.float32(1.0))
    rescale = children.shape[1] / child_mass
    return jnp.where(kept_mask[:, None], children * rescale[:, None], jnp.float32(0.0)).astype(jnp.bfloat16)


def bucket_sources(owners, kept_mask, devices, capacity):
    slot_count = owners.shape[0]
    onehot = ((owners[:, None] == jnp.arange(devices, dtype=jnp.int32)[None, :]) & kept_mask[:, None]).astype(jnp.int32)
    rank_owner = (jnp.sum(jnp.cumsum(onehot, axis=0).astype(jnp.int32) * onehot, axis=1) - 1).astype(jnp.int32)
    sent_mask = kept_mask & (rank_owner < capacity)
    destination = jnp.where(sent_mask, owners * capacity + rank_owner, devices * capacity).astype(jnp.int32)
    source = jnp.full((devices * capacity + 1,), slot_count, jnp.int32)
    source = source.at[destination].set(jnp.arange(slot_count, dtype=jnp.int32))
    return source[: devices * capacity]


def value_net(ranges, value_in, value_out):
    hidden = jnp.maximum(jnp.dot(ranges, value_in, preferred_element_type=jnp.float32), jnp.float32(0.0)).astype(jnp.bfloat16)
    return jnp.dot(hidden, value_out, preferred_element_type=jnp.float32).astype(jnp.bfloat16)


def reference(frontier, policy_table, first_counts, policy_index, owner_index, next_counts, value_in, value_out):
    devices = N_OWNER
    capacity = RECV_DEV // devices
    kept_limit = NODE_DEV * devices
    parents = frontier.reshape(devices, FRONT_DEV, HANDS)
    counts = first_counts.reshape(devices, FRONT_DEV)
    level_values = []
    for depth in range(LEVELS):
        policy_rows = policy_index[depth].reshape(devices, SLOTS)
        owner_rows = owner_index[depth].reshape(devices, SLOTS)
        if depth < LEVELS - 1:
            next_rows = next_counts[depth].reshape(devices, SLOTS)
        else:
            next_rows = jnp.zeros((devices, SLOTS), jnp.int32)
        totals = jax.vmap(lambda row: count_slots(row, SLOTS)[0])(counts).astype(jnp.int32)
        offsets = (jnp.cumsum(totals) - totals).astype(jnp.int32)

        def device_step(items):
            parent_block, count_block, policy_block, owner_block, next_block, offset = items
            child_total, slot_index, segment = count_slots(count_block, SLOTS)
            kept_mask = (slot_index < child_total) & (offset + slot_index < kept_limit)
            children = form_children(parent_block[segment], policy_table[policy_block], kept_mask)
            source = bucket_sources(owner_block, kept_mask, devices, capacity)
            padded_rows = jnp.concatenate([children, jnp.zeros((1, HANDS), jnp.bfloat16)], axis=0)
            padded_next = jnp.concatenate([next_block, jnp.zeros((1,), jnp.int32)])
            return padded_rows[source], padded_next[source]

        outgoing, outgoing_counts = lax.map(device_step, (parents, counts, policy_rows, owner_rows, next_rows, offsets))
        parents = outgoing.reshape(devices, devices, capacity, HANDS).transpose(1, 0, 2, 3).reshape(devices, devices * capacity, HANDS)
        counts = outgoing_counts.reshape(devices, devices, capacity).transpose(1, 0, 2).reshape(devices, devices * capacity)
        values = lax.map(lambda block: value_net(block, value_in, value_out), parents)
        level_values.append(values.reshape(devices * devices * capacity, HANDS))
    return jnp.stack(level_values)
```

```python
import jax
import jax.numpy as jnp
from jax import lax
from jax.sharding import PartitionSpec as P

LEVELS = 3
SLOTS = 512
RECV_DEV = 512
NODE_DEV = 384


def own_slots(owners, mine, capacity):
    slots = owners.shape[1]
    hit = owners == mine
    upper = jnp.triu(jnp.ones((slots, slots), jnp.bfloat16))
    count = jnp.dot(hit.astype(jnp.bfloat16), upper, preferred_element_type=jnp.float32).astype(
        jnp.int32
    )
    rank = jnp.where(hit, count - 1, -1)
    return rank[:, None, :] == jnp.arange(capacity, dtype=jnp.int32)[None, :, None]


def pick(onehot, values):
    return jnp.sum(jnp.where(onehot, values[:, None, :], 0), axis=2)


def gather_rows(table, index):
    onehot = index.reshape(-1)[:, None] == jnp.arange(table.shape[0], dtype=jnp.int32)[None, :]
    return jnp.dot(onehot.astype(jnp.bfloat16), table, preferred_element_type=jnp.float32)


def share(block):
    devices = lax.axis_size("owner")
    copies = jnp.broadcast_to(block[None], (devices,) + block.shape)
    return lax.all_to_all(copies, "owner", split_axis=0, concat_axis=0, tiled=True)


def on_device(
    frontier,
    policy_table,
    first_counts,
    policy_index,
    owner_index,
    next_counts,
    value_in,
    value_out,
):
    devices = lax.axis_size("owner")
    mine = lax.axis_index("owner")
    capacity = RECV_DEV // devices
    kept_limit = NODE_DEV * devices
    hands = frontier.shape[1]
    roots = share(frontier).reshape(-1, hands)
    meta = jnp.concatenate([owner_index, policy_index, next_counts], axis=0)
    meta = share(meta)
    counts = share(first_counts)
    lineage = [jnp.arange(roots.shape[0], dtype=jnp.int32).reshape(devices, -1)]
    level_values = []
    for depth in range(LEVELS):
        onehot = own_slots(meta[:, depth], mine, capacity)
        slot_index = jnp.arange(SLOTS, dtype=jnp.int32)[None, :]
        slot = pick(onehot, slot_index + 1) - 1
        policy = pick(onehot, meta[:, LEVELS + depth])
        ends = jnp.cumsum(counts, axis=1)
        totals = jnp.minimum(ends[:, -1], SLOTS)
        offsets = jnp.cumsum(totals) - totals
        kept = (slot >= 0) & (slot < totals[:, None]) & (offsets[:, None] + slot < kept_limit)
        parent = ((ends - counts)[:, None, :] <= slot[:, :, None]) & (
            slot[:, :, None] < ends[:, None, :]
        )
        lineage = [pick(parent, part) for part in lineage] + [policy]
        valid = kept.reshape(-1)
        rows = gather_rows(roots, jnp.where(kept, lineage[0], -1))
        for part in lineage[1:]:
            rows = rows * gather_rows(policy_table, part)
            mass = jnp.where(valid, jnp.sum(rows, axis=1), jnp.float32(1.0))
            rows = (rows * (hands / mass)[:, None]).astype(jnp.bfloat16).astype(jnp.float32)
        rows = rows.astype(jnp.bfloat16)
        hidden = jnp.maximum(
            jnp.dot(rows, value_in, preferred_element_type=jnp.float32), jnp.float32(0.0)
        ).astype(jnp.bfloat16)
        level_values.append(
            jnp.dot(hidden, value_out, preferred_element_type=jnp.float32).astype(jnp.bfloat16)
        )
        if depth < LEVELS - 1:
            following = jnp.where(kept, pick(onehot, meta[:, 2 * LEVELS + depth]), 0)
            packed = jnp.stack([part.reshape(-1) for part in lineage + [following]])
            packed = share(packed)
            lineage = [packed[:, k] for k in range(len(lineage))]
            counts = packed[:, -1]
    return jnp.stack(level_values)


def solution(mesh):
    placed = (
        P("owner", None),
        P(),
        P("owner"),
        P(None, "owner"),
        P(None, "owner"),
        P(None, "owner"),
        P(),
        P(),
    )
    return jax.shard_map(
        on_device, mesh=mesh, in_specs=placed, out_specs=P(None, "owner", None), check_vma=False
    )
```

```python
import jax
import jax.numpy as jnp
from jax import lax
from jax.experimental import pallas as pl
from jax.experimental.pallas import tpu as pltpu
from jax.sharding import PartitionSpec as P

LEVELS = 3
SLOTS = 512
RECV_DEV = 512
NODE_DEV = 384


def own_slots(owners, mine, capacity):
    slots = owners.shape[1]
    hit = owners == mine
    upper = jnp.triu(jnp.ones((slots, slots), jnp.bfloat16))
    count = jnp.dot(hit.astype(jnp.bfloat16), upper, preferred_element_type=jnp.float32).astype(
        jnp.int32
    )
    rank = jnp.where(hit, count - 1, -1)
    return rank[:, None, :] == jnp.arange(capacity, dtype=jnp.int32)[None, :, None]


def pick(onehot, values):
    return jnp.sum(jnp.where(onehot, values[:, None, :], 0), axis=2)


def step_place(step):
    level, begin = jnp.int32(0), jnp.int32(0)
    for depth in range(1, LEVELS):
        start = depth * (depth + 1) // 2
        level = jnp.where(step >= start, depth, level)
        begin = jnp.where(step >= start, start, begin)
    return level, step == begin, step == begin + level


def rebuild_kernel(
    index_ref,
    roots_hbm,
    table_hbm,
    in_hbm,
    out_hbm,
    values_ref,
    roots_ref,
    table_ref,
    in_ref,
    out_ref,
    rows_ref,
    sems,
):
    step = pl.program_id(0)
    level, first, last = step_place(step)
    copies = [
        pltpu.make_async_copy(source, target, sems.at[k])
        for k, (source, target) in enumerate(
            (
                (roots_hbm, roots_ref),
                (table_hbm, table_ref),
                (in_hbm, in_ref),
                (out_hbm, out_ref),
            )
        )
    ]

    @pl.when(step == 0)
    def _():
        for copy in copies:
            copy.start()
        copies[0].wait()
        copies[1].wait()

    index = index_ref[...]
    lane = lax.broadcasted_iota(jnp.int32, index.shape, 1)

    def column(place):
        return jnp.sum(jnp.where(lane == place, index, 0.0), axis=1, keepdims=True)

    def gathered(place, table):
        entry = lax.broadcasted_iota(jnp.int32, (index.shape[0], table.shape[0]), 1)
        onehot = jnp.where(entry.astype(jnp.float32) == column(place), 1.0, 0.0)
        return jnp.dot(
            onehot.astype(jnp.bfloat16), table[...], preferred_element_type=jnp.float32
        )

    root_place = LEVELS * (LEVELS + 1) // 2 + level

    @pl.when(first)
    def _():
        rows_ref[...] = gathered(root_place, roots_ref).astype(jnp.bfloat16)

    rows = rows_ref[...].astype(jnp.float32) * gathered(step, table_ref)
    mass = jnp.sum(rows, axis=1, keepdims=True)
    mass = jnp.where(column(root_place) >= 0.0, mass, 1.0)
    rows_ref[...] = (rows * (rows.shape[1] / mass)).astype(jnp.bfloat16)

    @pl.when(step == 0)
    def _():
        copies[2].wait()
        copies[3].wait()

    @pl.when(last)
    def _():
        hidden = jnp.dot(rows_ref[...], in_ref[...], preferred_element_type=jnp.float32)
        hidden = jnp.maximum(hidden, 0.0).astype(jnp.bfloat16)
        values = jnp.dot(hidden, out_ref[...], preferred_element_type=jnp.float32)
        values_ref[0] = values.astype(jnp.bfloat16)


def rebuild(index, roots, table, value_in, value_out):
    rows, hands = index.shape[0], table.shape[1]
    steps = LEVELS * (LEVELS + 1) // 2
    return pl.pallas_call(
        rebuild_kernel,
        grid=(steps,),
        out_shape=jax.ShapeDtypeStruct((LEVELS, rows, hands), jnp.bfloat16),
        in_specs=[pl.BlockSpec(index.shape, lambda step: (0, 0))]
        + [pl.BlockSpec(memory_space=pl.ANY)] * 4,
        out_specs=pl.BlockSpec((1, rows, hands), lambda step: (step_place(step)[0], 0, 0)),
        scratch_shapes=[
            pltpu.VMEM(array.shape, array.dtype) for array in (roots, table, value_in, value_out)
        ]
        + [pltpu.VMEM((rows, hands), jnp.bfloat16), pltpu.SemaphoreType.DMA((4,))],
        compiler_params=pltpu.CompilerParams(vmem_limit_bytes=56 * 1024 * 1024),
    )(index, roots, table, value_in, value_out)


def share(block):
    devices = lax.axis_size("owner")
    copies = jnp.broadcast_to(block[None], (devices,) + block.shape)
    return lax.all_to_all(copies, "owner", split_axis=0, concat_axis=0, tiled=True)


def on_device(
    frontier,
    policy_table,
    first_counts,
    policy_index,
    owner_index,
    next_counts,
    value_in,
    value_out,
):
    devices = lax.axis_size("owner")
    mine = lax.axis_index("owner")
    capacity = RECV_DEV // devices
    kept_limit = NODE_DEV * devices
    hands = frontier.shape[1]
    roots = share(frontier).reshape(-1, hands)
    meta = jnp.concatenate([owner_index, policy_index, next_counts], axis=0)
    meta = share(meta)
    counts = share(first_counts)
    lineage = [jnp.arange(roots.shape[0], dtype=jnp.int32).reshape(devices, -1)]
    columns, root_columns = [], []
    for depth in range(LEVELS):
        onehot = own_slots(meta[:, depth], mine, capacity)
        slot_index = jnp.arange(SLOTS, dtype=jnp.int32)[None, :]
        slot = pick(onehot, slot_index + 1) - 1
        policy = pick(onehot, meta[:, LEVELS + depth])
        ends = jnp.cumsum(counts, axis=1)
        totals = jnp.minimum(ends[:, -1], SLOTS)
        offsets = jnp.cumsum(totals) - totals
        kept = (slot >= 0) & (slot < totals[:, None]) & (offsets[:, None] + slot < kept_limit)
        parent = ((ends - counts)[:, None, :] <= slot[:, :, None]) & (
            slot[:, :, None] < ends[:, None, :]
        )
        lineage = [pick(parent, part) for part in lineage] + [policy]
        root_columns.append(jnp.where(kept, lineage[0], -1))
        columns += lineage[1:]
        if depth < LEVELS - 1:
            following = jnp.where(kept, pick(onehot, meta[:, 2 * LEVELS + depth]), 0)
            packed = jnp.stack([part.reshape(-1) for part in lineage + [following]])
            packed = share(packed)
            lineage = [packed[:, k] for k in range(len(lineage))]
            counts = packed[:, -1]
    index = jnp.stack([part.reshape(-1) for part in columns + root_columns], axis=1)
    return rebuild(index.astype(jnp.float32), roots, policy_table, value_in, value_out)


def solution(mesh):
    placed = (
        P("owner", None),
        P(),
        P("owner"),
        P(None, "owner"),
        P(None, "owner"),
        P(None, "owner"),
        P(),
        P(),
    )
    return jax.shard_map(
        on_device, mesh=mesh, in_specs=placed, out_specs=P(None, "owner", None), check_vma=False
    )
```

```python
import functools

import jax
import jax.numpy as jnp
from jax import lax
from jax.experimental import pallas as pl
from jax.experimental.pallas import tpu as pltpu
from jax.sharding import PartitionSpec as P

LEVELS = 3
SLOTS = 512
RECV_DEV = 512
NODE_DEV = 384
CORES = 2
PLANE = 8
HALF = 1 << 16
MESH = pl.DeviceIdType.MESH


def send_slots(owners, devices, capacity):
    slots = owners.shape[0]
    hit = owners[None, :] == jnp.arange(devices, dtype=jnp.int32)[:, None]
    upper = jnp.triu(jnp.ones((slots, slots), jnp.bfloat16))
    count = jnp.dot(hit.astype(jnp.bfloat16), upper, preferred_element_type=jnp.float32).astype(
        jnp.int32
    )
    rank = jnp.where(hit, count - 1, -1)
    return rank[:, None, :] == jnp.arange(capacity, dtype=jnp.int32)[None, :, None]


def pick(onehot, values):
    return jnp.sum(jnp.where(onehot, values[None, None, :], 0), axis=2)


def children_of(counts, slot):
    ends = jnp.cumsum(counts)
    parent = ((ends - counts)[None, None, :] <= slot[:, :, None]) & (
        slot[:, :, None] < ends[None, None, :]
    )
    return parent, jnp.minimum(ends[-1], SLOTS)


def step_place(step):
    level, begin = jnp.int32(0), jnp.int32(0)
    for depth in range(1, LEVELS):
        start = depth * (depth + 1) // 2
        level = jnp.where(step >= start, depth, level)
        begin = jnp.where(step >= start, start, begin)
    return level, step == begin, step == begin + level


def dot_last(left, right):
    return lax.dot_general(
        left, right, (((1,), (1,)), ((), ())), preferred_element_type=jnp.float32
    )


def rebuild_kernel(
    index_ref,
    roots_hbm,
    table_hbm,
    in_hbm,
    out_hbm,
    values_ref,
    roots_ref,
    table_ref,
    in_ref,
    out_ref,
    rows_ref,
    sems,
):
    step = pl.program_id(0)
    level, first, last = step_place(step)
    copies = [
        pltpu.make_async_copy(source, target, sems.at[k])
        for k, (source, target) in enumerate(
            (
                (roots_hbm, roots_ref),
                (table_hbm, table_ref),
                (in_hbm, in_ref),
                (out_hbm, out_ref),
            )
        )
    ]

    @pl.when(step == 0)
    def _():
        for copy in copies:
            copy.start()
        copies[0].wait()
        copies[1].wait()

    index = index_ref[...]
    lane = lax.broadcasted_iota(jnp.int32, index.shape, 1)

    def column(place):
        return jnp.sum(jnp.where(lane == place, index, 0.0), axis=1, keepdims=True)

    def picked(place, entries):
        entry = lax.broadcasted_iota(jnp.int32, (index.shape[0], entries), 1)
        onehot = jnp.where(entry.astype(jnp.float32) == column(place), 1.0, 0.0)
        return onehot.astype(jnp.bfloat16)

    root_place = LEVELS * (LEVELS + 1) // 2 + level

    @pl.when(first)
    def _():
        rows_ref[...] = jnp.dot(
            picked(root_place, roots_ref.shape[0]),
            roots_ref[...],
            preferred_element_type=jnp.float32,
        ).astype(jnp.bfloat16)

    rows = rows_ref[...].astype(jnp.float32) * dot_last(
        picked(step, table_ref.shape[1]), table_ref[...]
    )
    mass = jnp.sum(rows, axis=1, keepdims=True)
    mass = jnp.where(column(root_place) >= 0.0, mass, 1.0)
    rows_ref[...] = (rows * (rows.shape[1] / mass)).astype(jnp.bfloat16)

    @pl.when(step == 0)
    def _():
        copies[2].wait()
        copies[3].wait()

    @pl.when(last)
    def _():
        hidden = jnp.dot(rows_ref[...], in_ref[...], preferred_element_type=jnp.float32)
        hidden = jnp.maximum(hidden, 0.0).astype(jnp.bfloat16)
        values_ref[0] = dot_last(out_ref[...], hidden).astype(jnp.bfloat16)


def rebuild(index, roots, table, value_in, value_out):
    rows, hands = index.shape[0], table.shape[0]
    steps = LEVELS * (LEVELS + 1) // 2
    return pl.pallas_call(
        rebuild_kernel,
        grid=(steps,),
        out_shape=jax.ShapeDtypeStruct((LEVELS, hands, rows), jnp.bfloat16),
        in_specs=[pl.BlockSpec(index.shape, lambda step: (0, 0))]
        + [pl.BlockSpec(memory_space=pl.ANY)] * 4,
        out_specs=pl.BlockSpec((1, hands, rows), lambda step: (step_place(step)[0], 0, 0)),
        scratch_shapes=[
            pltpu.VMEM(array.shape, array.dtype) for array in (roots, table, value_in, value_out)
        ]
        + [pltpu.VMEM((rows, hands), jnp.bfloat16), pltpu.SemaphoreType.DMA((4,))],
        compiler_params=pltpu.CompilerParams(vmem_limit_bytes=56 * 1024 * 1024),
    )(index, roots, table, value_in, value_out)


def place_of(mine):
    return mine // PLANE, mine % PLANE // CORES, mine % CORES


def exchange_kernel(devices, stage, notes_ref, rows_ref, out_notes_ref, out_rows_ref, *sems):
    note_send, note_recv, row_send, row_recv, own_sem = sems
    mine = lax.axis_index("owner")
    line, chip, core = place_of(mine)

    barrier = pltpu.get_barrier_semaphore()

    @pl.loop(1, devices)
    def _(turn):
        peer = lax.rem(mine + turn, devices)
        pl.semaphore_signal(barrier, inc=1, device_id=(peer,), device_id_type=MESH)

    pl.semaphore_wait(barrier, devices - 1)

    def note(turn):
        peer = lax.rem(mine + turn, devices)
        return pltpu.make_async_remote_copy(
            src_ref=notes_ref.at[peer],
            dst_ref=out_notes_ref.at[mine],
            send_sem=note_send.at[turn - 1],
            recv_sem=note_recv.at[turn - 1],
            device_id=(peer,),
            device_id_type=MESH,
        )

    @pl.loop(1, devices)
    def _(turn):
        note(turn).start()

    parts = out_rows_ref.shape[0]
    slot = (line, chip, core)[stage]
    moves = []
    for turn in range(1, parts):
        other = lax.rem(slot + turn, parts)
        peer = (
            other * PLANE + mine % PLANE,
            line * PLANE + other * CORES + core,
            line * PLANE + chip * CORES + other,
        )[stage]
        moves.append(
            pltpu.make_async_remote_copy(
                src_ref=rows_ref,
                dst_ref=out_rows_ref.at[slot],
                send_sem=row_send.at[turn - 1],
                recv_sem=row_recv.at[turn - 1],
                device_id=(peer,),
                device_id_type=MESH,
            )
        )
    for move in moves:
        move.start()
    own = (
        pltpu.make_async_copy(notes_ref.at[mine], out_notes_ref.at[mine], own_sem.at[0]),
        pltpu.make_async_copy(rows_ref, out_rows_ref.at[slot], own_sem.at[1]),
    )
    for copy in own:
        copy.start()

    @pl.loop(1, devices)
    def _(turn):
        note(turn).wait()

    for move in moves:
        move.wait()
    for copy in own:
        copy.wait()


def exchange(stage, notes, rows):
    devices = lax.axis_size("owner")
    parts = (devices // PLANE, PLANE // CORES, CORES)[stage]
    width = -(-notes.shape[1] // 128) * 128
    notes = jnp.pad(notes, ((0, 0), (0, width - notes.shape[1])))[:, None, :]
    out_notes, out_rows = pl.pallas_call(
        functools.partial(exchange_kernel, devices, stage),
        out_shape=(
            jax.ShapeDtypeStruct(notes.shape, notes.dtype),
            jax.ShapeDtypeStruct((parts,) + rows.shape, rows.dtype),
        ),
        in_specs=[pl.BlockSpec(memory_space=pltpu.VMEM)] * 2,
        out_specs=(pl.BlockSpec(memory_space=pltpu.VMEM),) * 2,
        scratch_shapes=[
            pltpu.SemaphoreType.DMA((devices - 1,)),
            pltpu.SemaphoreType.DMA((devices - 1,)),
            pltpu.SemaphoreType.DMA((max(parts - 1, 1),)),
            pltpu.SemaphoreType.DMA((max(parts - 1, 1),)),
            pltpu.SemaphoreType.DMA((2,)),
        ],
        compiler_params=pltpu.CompilerParams(collective_id=stage, has_side_effects=True),
    )(notes, rows)
    return out_notes[:, 0, :], out_rows


def on_device(
    frontier,
    policy_table,
    first_counts,
    policy_index,
    owner_index,
    next_counts,
    value_in,
    value_out,
):
    devices = lax.axis_size("owner")
    mine = lax.axis_index("owner")
    capacity = RECV_DEV // devices
    kept_limit = NODE_DEV * devices
    line, chip, core = place_of(mine)
    lines, chips = devices // PLANE, PLANE // CORES
    first_root = ((core * chips + chip) * lines + line) * frontier.shape[0]
    onehots = [send_slots(owner_index[depth], devices, capacity) for depth in range(LEVELS)]
    slot_index = jnp.arange(SLOTS, dtype=jnp.int32)
    slots = [pick(onehot, slot_index + 1) - 1 for onehot in onehots]
    notes = list(slots)
    for depth in range(LEVELS):
        value = policy_index[depth]
        if depth < LEVELS - 1:
            value = value + HALF * next_counts[depth]
        notes.append(pick(onehots[depth], value))
    lineage = [first_root + jnp.arange(frontier.shape[0], dtype=jnp.int32)]
    counts = first_counts
    rows = frontier
    columns, root_columns = [], []
    for depth in range(LEVELS):
        parent, total = children_of(counts, slots[depth])
        notes += [pick(parent, part) for part in lineage]
        notes.append(jnp.broadcast_to(total, (devices, 1)))
        received, rows = exchange(depth, jnp.concatenate(notes, axis=1), rows)
        if depth == 0:
            first = [
                received[:, k * capacity : (k + 1) * capacity] for k in range(2 * LEVELS)
            ]
            received = received[:, 2 * LEVELS * capacity :]
        lineage = [
            received[:, k * capacity : (k + 1) * capacity] for k in range(len(lineage))
        ]
        totals = received[:, len(lineage) * capacity]
        offsets = jnp.cumsum(totals) - totals
        slot = first[depth]
        policy = first[LEVELS + depth] % HALF
        kept = (slot >= 0) & (slot < totals[:, None]) & (offsets[:, None] + slot < kept_limit)
        if depth == 0:
            path = lineage + [policy]
        elif depth == 1:
            path = [lineage[0] % HALF, lineage[0] // HALF, policy]
        else:
            path = [lineage[0] % HALF, lineage[0] // HALF, lineage[1], policy]
        root_columns.append(jnp.where(kept, path[0], -1))
        columns += path[1:]
        counts = jnp.where(kept, first[LEVELS + depth] // HALF, 0).reshape(-1)
        path = [part.reshape(-1) for part in path]
        lineage = [path[0] + HALF * path[1]] + path[2:]
        notes = []
    roots = rows.reshape(-1, rows.shape[-1])
    index = jnp.stack([part.reshape(-1) for part in columns + root_columns], axis=1)
    values = rebuild(
        index.astype(jnp.float32), roots, policy_table.T, value_in, value_out.T
    )
    return jnp.swapaxes(values, 1, 2)


def solution(mesh):
    placed = (
        P("owner", None),
        P(),
        P("owner"),
        P(None, "owner"),
        P(None, "owner"),
        P(None, "owner"),
        P(),
        P(),
    )
    return jax.shard_map(
        on_device, mesh=mesh, in_specs=placed, out_specs=P(None, "owner", None), check_vma=False
    )
```

```python
import functools

import jax
import jax.numpy as jnp
from jax import lax
from jax.experimental import pallas as pl
from jax.experimental.pallas import tpu as pltpu
from jax.sharding import PartitionSpec as P

LEVELS = 3
SLOTS = 512
RECV_DEV = 512
NODE_DEV = 384
CORES = 2
PLANE = 8
HALF = 1 << 16
MESH = pl.DeviceIdType.MESH


def send_slots(owners, devices, capacity):
    slots = owners.shape[0]
    hit = owners[None, :] == jnp.arange(devices, dtype=jnp.int32)[:, None]
    upper = jnp.triu(jnp.ones((slots, slots), jnp.bfloat16))
    count = jnp.dot(hit.astype(jnp.bfloat16), upper, preferred_element_type=jnp.float32).astype(
        jnp.int32
    )
    rank = jnp.where(hit, count - 1, -1)
    return rank[:, None, :] == jnp.arange(capacity, dtype=jnp.int32)[None, :, None]


def pick(onehot, values):
    return jnp.sum(jnp.where(onehot, values[None, None, :], 0), axis=2)


def children_of(counts, slot):
    ends = jnp.cumsum(counts)
    parent = ((ends - counts)[None, None, :] <= slot[:, :, None]) & (
        slot[:, :, None] < ends[None, None, :]
    )
    return parent, jnp.minimum(ends[-1], SLOTS)


def step_place(step):
    level, begin = jnp.int32(0), jnp.int32(0)
    for depth in range(1, LEVELS):
        start = depth * (depth + 1) // 2
        level = jnp.where(step >= start, depth, level)
        begin = jnp.where(step >= start, start, begin)
    return level, step == begin, step == begin + level


def dot_last(left, right):
    return lax.dot_general(
        left, right, (((1,), (1,)), ((), ())), preferred_element_type=jnp.float32
    )


def column_of(index, place):
    lane = lax.broadcasted_iota(jnp.int32, index.shape, 1)
    return jnp.sum(jnp.where(lane == place, index, 0.0), axis=1, keepdims=True)


def picked(index, place, entries):
    entry = lax.broadcasted_iota(jnp.int32, (index.shape[0], entries), 1)
    onehot = jnp.where(entry.astype(jnp.float32) == column_of(index, place), 1.0, 0.0)
    return onehot.astype(jnp.bfloat16)


def rebuild_kernel(
    index_ref,
    policy_ref,
    roots_hbm,
    table_hbm,
    in_hbm,
    out_hbm,
    values_ref,
    roots_ref,
    table_ref,
    in_ref,
    out_ref,
    rows_ref,
    factor_ref,
    sems,
):
    step = pl.program_id(0)
    level, first, last = step_place(step)
    copies = [
        pltpu.make_async_copy(source, target, sems.at[k])
        for k, (source, target) in enumerate(
            (
                (roots_hbm, roots_ref),
                (in_hbm, in_ref),
                (out_hbm, out_ref),
                (table_hbm, table_ref),
            )
        )
    ]

    @pl.when(step == 0)
    def _():
        for copy in copies:
            copy.start()
        copies[0].wait()

    @pl.when(step == 1)
    def _():
        copies[3].wait()

    index = index_ref[...]
    root_place = LEVELS * (LEVELS + 1) // 2 + level

    @pl.when(first)
    def _():
        rows_ref[...] = jnp.dot(
            picked(index, root_place, roots_ref.shape[0]),
            roots_ref[...],
            preferred_element_type=jnp.float32,
        ).astype(jnp.bfloat16)

    @pl.when(last)
    def _():
        factor_ref[...] = policy_ref[0]

    @pl.when(jnp.logical_not(last))
    def _():
        factor = dot_last(picked(index, step, table_ref.shape[1]), table_ref[...])
        factor_ref[...] = factor.astype(jnp.bfloat16)

    rows = rows_ref[...].astype(jnp.float32) * factor_ref[...].astype(jnp.float32)
    mass = jnp.sum(rows, axis=1, keepdims=True)
    mass = jnp.where(column_of(index, root_place) >= 0.0, mass, 1.0)
    rows_ref[...] = (rows * (rows.shape[1] / mass)).astype(jnp.bfloat16)

    @pl.when(step == 0)
    def _():
        copies[1].wait()
        copies[2].wait()

    @pl.when(last)
    def _():
        hidden = jnp.dot(rows_ref[...], in_ref[...], preferred_element_type=jnp.float32)
        hidden = jnp.maximum(hidden, 0.0).astype(jnp.bfloat16)
        values_ref[0] = dot_last(out_ref[...], hidden).astype(jnp.bfloat16)


def rebuild(index, policy_rows, roots, table, value_in, value_out):
    rows, hands = index.shape[0], table.shape[0]
    steps = LEVELS * (LEVELS + 1) // 2
    return pl.pallas_call(
        rebuild_kernel,
        grid=(steps,),
        out_shape=jax.ShapeDtypeStruct((LEVELS, hands, rows), jnp.bfloat16),
        in_specs=[
            pl.BlockSpec(index.shape, lambda step: (0, 0)),
            pl.BlockSpec((1, rows, hands), lambda step: (step_place(step)[0], 0, 0)),
        ]
        + [pl.BlockSpec(memory_space=pl.ANY)] * 4,
        out_specs=pl.BlockSpec((1, hands, rows), lambda step: (step_place(step)[0], 0, 0)),
        scratch_shapes=[
            pltpu.VMEM(array.shape, array.dtype) for array in (roots, table, value_in, value_out)
        ]
        + [pltpu.VMEM((rows, hands), jnp.bfloat16)] * 2
        + [pltpu.SemaphoreType.DMA((4,))],
        compiler_params=pltpu.CompilerParams(vmem_limit_bytes=56 * 1024 * 1024),
    )(index, policy_rows, roots, table, value_in, value_out)


def place_of(mine):
    return mine // PLANE, mine % PLANE // CORES, mine % CORES


def exchange_kernel(devices, stage, *refs):
    if len(refs) == 9:
        notes_ref, rows_ref, out_notes_ref, out_rows_ref = refs[:4]
    else:
        notes_ref, rows_ref, index_ref, table_hbm, out_notes_ref, out_rows_ref, policy_hbm = refs[:7]
        table_ref, policy_ref, policy_sem = refs[12:]
        refs = refs[3:12]
        load = pltpu.make_async_copy(table_hbm, table_ref, policy_sem.at[LEVELS])
        load.start()
    note_send, note_recv, row_send, row_recv, own_sem = refs[4:9]
    mine = lax.axis_index("owner")
    line, chip, core = place_of(mine)

    barrier = pltpu.get_barrier_semaphore()

    @pl.loop(1, devices)
    def _(turn):
        peer = lax.rem(mine + turn, devices)
        pl.semaphore_signal(barrier, inc=1, device_id=(peer,), device_id_type=MESH)

    pl.semaphore_wait(barrier, devices - 1)

    def note(turn):
        peer = lax.rem(mine + turn, devices)
        return pltpu.make_async_remote_copy(
            src_ref=notes_ref.at[peer],
            dst_ref=out_notes_ref.at[mine],
            send_sem=note_send.at[turn - 1],
            recv_sem=note_recv.at[turn - 1],
            device_id=(peer,),
            device_id_type=MESH,
        )

    @pl.loop(1, devices)
    def _(turn):
        note(turn).start()

    parts = out_rows_ref.shape[0]
    slot = (line, chip, core)[stage]
    moves = []
    for turn in range(1, parts):
        other = lax.rem(slot + turn, parts)
        peer = (
            other * PLANE + mine % PLANE,
            line * PLANE + other * CORES + core,
            line * PLANE + chip * CORES + other,
        )[stage]
        moves.append(
            pltpu.make_async_remote_copy(
                src_ref=rows_ref,
                dst_ref=out_rows_ref.at[slot],
                send_sem=row_send.at[turn - 1],
                recv_sem=row_recv.at[turn - 1],
                device_id=(peer,),
                device_id_type=MESH,
            )
        )
    for move in moves:
        move.start()
    own = (
        pltpu.make_async_copy(notes_ref.at[mine], out_notes_ref.at[mine], own_sem.at[0]),
        pltpu.make_async_copy(rows_ref, out_rows_ref.at[slot], own_sem.at[1]),
    )
    for copy in own:
        copy.start()

    if stage == 1:
        load.wait()

        def store(depth):
            return pltpu.make_async_copy(
                policy_ref.at[depth], policy_hbm.at[depth], policy_sem.at[depth]
            )

        @pl.loop(0, LEVELS)
        def _(depth):
            onehot = picked(index_ref[...], depth, table_ref.shape[1])
            policy_ref[depth] = dot_last(onehot, table_ref[...]).astype(jnp.bfloat16)
            store(depth).start()

        for depth in range(LEVELS):
            store(depth).wait()

    @pl.loop(1, devices)
    def _(turn):
        note(turn).wait()

    for move in moves:
        move.wait()
    for copy in own:
        copy.wait()


def exchange(stage, notes, rows, extra=()):
    devices = lax.axis_size("owner")
    parts = (devices // PLANE, PLANE // CORES, CORES)[stage]
    width = -(-notes.shape[1] // 128) * 128
    notes = jnp.pad(notes, ((0, 0), (0, width - notes.shape[1])))[:, None, :]
    vmem, anywhere = pl.BlockSpec(memory_space=pltpu.VMEM), pl.BlockSpec(memory_space=pl.ANY)
    out_shape = [
        jax.ShapeDtypeStruct(notes.shape, notes.dtype),
        jax.ShapeDtypeStruct((parts,) + rows.shape, rows.dtype),
    ]
    in_specs, out_specs = [vmem, vmem], [vmem, vmem]
    scratch = [
        pltpu.SemaphoreType.DMA((devices - 1,)),
        pltpu.SemaphoreType.DMA((devices - 1,)),
        pltpu.SemaphoreType.DMA((max(parts - 1, 1),)),
        pltpu.SemaphoreType.DMA((max(parts - 1, 1),)),
        pltpu.SemaphoreType.DMA((2,)),
    ]
    if extra:
        index, table = extra
        shape = (LEVELS, index.shape[0], table.shape[0])
        out_shape.append(jax.ShapeDtypeStruct(shape, table.dtype))
        in_specs += [vmem, anywhere]
        out_specs.append(anywhere)
        scratch += [
            pltpu.VMEM(table.shape, table.dtype),
            pltpu.VMEM(shape, table.dtype),
            pltpu.SemaphoreType.DMA((LEVELS + 1,)),
        ]
    out = pl.pallas_call(
        functools.partial(exchange_kernel, devices, stage),
        out_shape=out_shape,
        in_specs=in_specs,
        out_specs=out_specs,
        scratch_shapes=scratch,
        compiler_params=pltpu.CompilerParams(
            collective_id=stage, has_side_effects=True, vmem_limit_bytes=48 * 1024 * 1024
        ),
    )(notes, rows, *extra)
    return (out[0][:, 0, :],) + tuple(out[1:])


def on_device(
    frontier,
    policy_table,
    first_counts,
    policy_index,
    owner_index,
    next_counts,
    value_in,
    value_out,
):
    devices = lax.axis_size("owner")
    mine = lax.axis_index("owner")
    capacity = RECV_DEV // devices
    kept_limit = NODE_DEV * devices
    line, chip, core = place_of(mine)
    lines, chips = devices // PLANE, PLANE // CORES
    first_root = ((core * chips + chip) * lines + line) * frontier.shape[0]
    onehots = [send_slots(owner_index[depth], devices, capacity) for depth in range(LEVELS)]
    slot_index = jnp.arange(SLOTS, dtype=jnp.int32)
    slots = [pick(onehot, slot_index + 1) - 1 for onehot in onehots]
    notes = list(slots)
    for depth in range(LEVELS):
        value = policy_index[depth]
        if depth < LEVELS - 1:
            value = value + HALF * next_counts[depth]
        notes.append(pick(onehots[depth], value))
    lineage = [first_root + jnp.arange(frontier.shape[0], dtype=jnp.int32)]
    counts = first_counts
    rows = frontier
    columns, root_columns = [], []
    for depth in range(LEVELS):
        parent, total = children_of(counts, slots[depth])
        notes += [pick(parent, part) for part in lineage]
        notes.append(jnp.broadcast_to(total, (devices, 1)))
        notes = jnp.concatenate(notes, axis=1)
        if depth == 1:
            last_index = jnp.stack(
                [(part % HALF).reshape(-1) for part in first[LEVELS:]], axis=1
            ).astype(jnp.float32)
            received, rows, policy_rows = exchange(
                depth, notes, rows, (last_index, policy_table.T)
            )
        else:
            received, rows = exchange(depth, notes, rows)
        if depth == 0:
            first = [
                received[:, k * capacity : (k + 1) * capacity] for k in range(2 * LEVELS)
            ]
            received = received[:, 2 * LEVELS * capacity :]
        lineage = [
            received[:, k * capacity : (k + 1) * capacity] for k in range(len(lineage))
        ]
        totals = received[:, len(lineage) * capacity]
        offsets = jnp.cumsum(totals) - totals
        slot = first[depth]
        policy = first[LEVELS + depth] % HALF
        kept = (slot >= 0) & (slot < totals[:, None]) & (offsets[:, None] + slot < kept_limit)
        if depth == 0:
            path = lineage + [policy]
        elif depth == 1:
            path = [lineage[0] % HALF, lineage[0] // HALF, policy]
        else:
            path = [lineage[0] % HALF, lineage[0] // HALF, lineage[1], policy]
        root_columns.append(jnp.where(kept, path[0], -1))
        columns += path[1:]
        counts = jnp.where(kept, first[LEVELS + depth] // HALF, 0).reshape(-1)
        path = [part.reshape(-1) for part in path]
        lineage = [path[0] + HALF * path[1]] + path[2:]
        notes = []
    roots = rows.reshape(-1, rows.shape[-1])
    index = jnp.stack([part.reshape(-1) for part in columns + root_columns], axis=1)
    values = rebuild(
        index.astype(jnp.float32), policy_rows, roots, policy_table.T, value_in, value_out.T
    )
    return jnp.swapaxes(values, 1, 2)


def solution(mesh):
    placed = (
        P("owner", None),
        P(),
        P("owner"),
        P(None, "owner"),
        P(None, "owner"),
        P(None, "owner"),
        P(),
        P(),
    )
    return jax.shard_map(
        on_device, mesh=mesh, in_specs=placed, out_specs=P(None, "owner", None), check_vma=False
    )
```

```python
import functools

import jax
import jax.numpy as jnp
from jax import lax
from jax.experimental import pallas as pl
from jax.experimental.pallas import tpu as pltpu
from jax.sharding import PartitionSpec as P

LEVELS = 3
SLOTS = 512
RECV_DEV = 512
NODE_DEV = 384
CORES = 2
PLANE = 8
HALF = 1 << 16
MESH = pl.DeviceIdType.MESH


def send_slots(owners, devices, capacity):
    slots = owners.shape[0]
    hit = owners[None, :] == jnp.arange(devices, dtype=jnp.int32)[:, None]
    upper = jnp.triu(jnp.ones((slots, slots), jnp.bfloat16))
    count = jnp.dot(hit.astype(jnp.bfloat16), upper, preferred_element_type=jnp.float32).astype(
        jnp.int32
    )
    rank = jnp.where(hit, count - 1, -1)
    return rank[:, None, :] == jnp.arange(capacity, dtype=jnp.int32)[None, :, None]


def pick(onehot, values):
    return jnp.sum(jnp.where(onehot, values[None, None, :], 0), axis=2)


def children_of(counts, slot):
    ends = jnp.cumsum(counts)
    parent = ((ends - counts)[None, None, :] <= slot[:, :, None]) & (
        slot[:, :, None] < ends[None, None, :]
    )
    return parent, jnp.minimum(ends[-1], SLOTS)


def step_place(step):
    level, begin = jnp.int32(0), jnp.int32(0)
    for depth in range(1, LEVELS):
        start = depth * (depth + 1) // 2
        level = jnp.where(step >= start, depth, level)
        begin = jnp.where(step >= start, start, begin)
    return level, step == begin, step == begin + level


def dot_last(left, right):
    return lax.dot_general(
        left, right, (((1,), (1,)), ((), ())), preferred_element_type=jnp.float32
    )


def column_of(index, place):
    lane = lax.broadcasted_iota(jnp.int32, index.shape, 1)
    return jnp.sum(jnp.where(lane == place, index, 0.0), axis=1, keepdims=True)


def picked(index, place, entries):
    entry = lax.broadcasted_iota(jnp.int32, (index.shape[0], entries), 1)
    onehot = jnp.where(entry.astype(jnp.float32) == column_of(index, place), 1.0, 0.0)
    return onehot.astype(jnp.bfloat16)


def rebuild_kernel(
    index_ref,
    policy_ref,
    second_ref,
    roots_hbm,
    table_hbm,
    in_hbm,
    out_hbm,
    values_ref,
    roots_ref,
    table_ref,
    in_ref,
    out_ref,
    rows_ref,
    factor_ref,
    sems,
):
    step = pl.program_id(0)
    level, first, last = step_place(step)
    copies = [
        pltpu.make_async_copy(source, target, sems.at[k])
        for k, (source, target) in enumerate(
            (
                (roots_hbm, roots_ref),
                (in_hbm, in_ref),
                (out_hbm, out_ref),
                (table_hbm, table_ref),
            )
        )
    ]

    @pl.when(step == 0)
    def _():
        for copy in copies:
            copy.start()
        copies[0].wait()

    @pl.when(step == 3)
    def _():
        copies[3].wait()

    index = index_ref[...]
    root_place = LEVELS * (LEVELS + 1) // 2 + level

    @pl.when(first)
    def _():
        rows_ref[...] = jnp.dot(
            picked(index, root_place, roots_ref.shape[0]),
            roots_ref[...],
            preferred_element_type=jnp.float32,
        ).astype(jnp.bfloat16)

    @pl.when(last)
    def _():
        factor_ref[...] = policy_ref[0]

    @pl.when(step == 1)
    def _():
        factor_ref[...] = second_ref[0]

    @pl.when(jnp.logical_not(last) & (step > 1))
    def _():
        factor = dot_last(picked(index, step, table_ref.shape[1]), table_ref[...])
        factor_ref[...] = factor.astype(jnp.bfloat16)

    rows = rows_ref[...].astype(jnp.float32) * factor_ref[...].astype(jnp.float32)
    mass = jnp.sum(rows, axis=1, keepdims=True)
    mass = jnp.where(column_of(index, root_place) >= 0.0, mass, 1.0)
    rows_ref[...] = (rows * (rows.shape[1] / mass)).astype(jnp.bfloat16)

    @pl.when(step == 0)
    def _():
        copies[1].wait()
        copies[2].wait()

    @pl.when(last)
    def _():
        hidden = jnp.dot(rows_ref[...], in_ref[...], preferred_element_type=jnp.float32)
        hidden = jnp.maximum(hidden, 0.0).astype(jnp.bfloat16)
        values_ref[0] = dot_last(out_ref[...], hidden).astype(jnp.bfloat16)


def rebuild(index, policy_rows, second_rows, roots, table, value_in, value_out):
    rows, hands = index.shape[0], table.shape[0]
    steps = LEVELS * (LEVELS + 1) // 2
    return pl.pallas_call(
        rebuild_kernel,
        grid=(steps,),
        out_shape=jax.ShapeDtypeStruct((LEVELS, hands, rows), jnp.bfloat16),
        in_specs=[
            pl.BlockSpec(index.shape, lambda step: (0, 0)),
            pl.BlockSpec((1, rows, hands), lambda step: (step_place(step)[0], 0, 0)),
            pl.BlockSpec((1, rows, hands), lambda step: (0, 0, 0)),
        ]
        + [pl.BlockSpec(memory_space=pl.ANY)] * 4,
        out_specs=pl.BlockSpec((1, hands, rows), lambda step: (step_place(step)[0], 0, 0)),
        scratch_shapes=[
            pltpu.VMEM(array.shape, array.dtype) for array in (roots, table, value_in, value_out)
        ]
        + [pltpu.VMEM((rows, hands), jnp.bfloat16)] * 2
        + [pltpu.SemaphoreType.DMA((4,))],
        compiler_params=pltpu.CompilerParams(vmem_limit_bytes=56 * 1024 * 1024),
    )(index, policy_rows, second_rows, roots, table, value_in, value_out)


def place_of(mine):
    return mine // PLANE, mine % PLANE // CORES, mine % CORES


def exchange_kernel(devices, stage, *refs):
    if len(refs) == 9:
        notes_ref, rows_ref, out_notes_ref, out_rows_ref = refs[:4]
    else:
        notes_ref, rows_ref, index_ref, table_hbm, out_notes_ref, out_rows_ref, policy_hbm = refs[:7]
        table_ref, policy_ref, policy_sem = refs[12:]
        refs = refs[3:12]
        load = pltpu.make_async_copy(table_hbm, table_ref, policy_sem.at[policy_ref.shape[0]])
        load.start()
    note_send, note_recv, row_send, row_recv, own_sem = refs[4:9]
    mine = lax.axis_index("owner")
    line, chip, core = place_of(mine)

    barrier = pltpu.get_barrier_semaphore()

    @pl.loop(1, devices)
    def _(turn):
        peer = lax.rem(mine + turn, devices)
        pl.semaphore_signal(barrier, inc=1, device_id=(peer,), device_id_type=MESH)

    pl.semaphore_wait(barrier, devices - 1)

    def note(turn):
        peer = lax.rem(mine + turn, devices)
        return pltpu.make_async_remote_copy(
            src_ref=notes_ref.at[peer],
            dst_ref=out_notes_ref.at[mine],
            send_sem=note_send.at[turn - 1],
            recv_sem=note_recv.at[turn - 1],
            device_id=(peer,),
            device_id_type=MESH,
        )

    @pl.loop(1, devices)
    def _(turn):
        note(turn).start()

    parts = out_rows_ref.shape[0]
    slot = (line, chip, core)[stage]
    moves = []
    for turn in range(1, parts):
        other = lax.rem(slot + turn, parts)
        peer = (
            other * PLANE + mine % PLANE,
            line * PLANE + other * CORES + core,
            line * PLANE + chip * CORES + other,
        )[stage]
        moves.append(
            pltpu.make_async_remote_copy(
                src_ref=rows_ref,
                dst_ref=out_rows_ref.at[slot],
                send_sem=row_send.at[turn - 1],
                recv_sem=row_recv.at[turn - 1],
                device_id=(peer,),
                device_id_type=MESH,
            )
        )
    for move in moves:
        move.start()
    own = (
        pltpu.make_async_copy(notes_ref.at[mine], out_notes_ref.at[mine], own_sem.at[0]),
        pltpu.make_async_copy(rows_ref, out_rows_ref.at[slot], own_sem.at[1]),
    )
    for copy in own:
        copy.start()

    if stage > 0:
        picks = policy_ref.shape[0]
        load.wait()

        def store(depth):
            return pltpu.make_async_copy(
                policy_ref.at[depth], policy_hbm.at[depth], policy_sem.at[depth]
            )

        @pl.loop(0, picks)
        def _(depth):
            onehot = picked(index_ref[...], depth, table_ref.shape[1])
            policy_ref[depth] = dot_last(onehot, table_ref[...]).astype(jnp.bfloat16)
            store(depth).start()

        for depth in range(picks):
            store(depth).wait()

    @pl.loop(1, devices)
    def _(turn):
        note(turn).wait()

    for move in moves:
        move.wait()
    for copy in own:
        copy.wait()


def exchange(stage, notes, rows, extra=()):
    devices = lax.axis_size("owner")
    parts = (devices // PLANE, PLANE // CORES, CORES)[stage]
    width = -(-notes.shape[1] // 128) * 128
    notes = jnp.pad(notes, ((0, 0), (0, width - notes.shape[1])))[:, None, :]
    vmem, anywhere = pl.BlockSpec(memory_space=pltpu.VMEM), pl.BlockSpec(memory_space=pl.ANY)
    out_shape = [
        jax.ShapeDtypeStruct(notes.shape, notes.dtype),
        jax.ShapeDtypeStruct((parts,) + rows.shape, rows.dtype),
    ]
    in_specs, out_specs = [vmem, vmem], [vmem, vmem]
    scratch = [
        pltpu.SemaphoreType.DMA((devices - 1,)),
        pltpu.SemaphoreType.DMA((devices - 1,)),
        pltpu.SemaphoreType.DMA((max(parts - 1, 1),)),
        pltpu.SemaphoreType.DMA((max(parts - 1, 1),)),
        pltpu.SemaphoreType.DMA((2,)),
    ]
    if extra:
        index, table = extra
        shape = (index.shape[1], index.shape[0], table.shape[0])
        out_shape.append(jax.ShapeDtypeStruct(shape, table.dtype))
        in_specs += [vmem, anywhere]
        out_specs.append(anywhere)
        scratch += [
            pltpu.VMEM(table.shape, table.dtype),
            pltpu.VMEM(shape, table.dtype),
            pltpu.SemaphoreType.DMA((index.shape[1] + 1,)),
        ]
    out = pl.pallas_call(
        functools.partial(exchange_kernel, devices, stage),
        out_shape=out_shape,
        in_specs=in_specs,
        out_specs=out_specs,
        scratch_shapes=scratch,
        compiler_params=pltpu.CompilerParams(
            collective_id=stage, has_side_effects=True, vmem_limit_bytes=48 * 1024 * 1024
        ),
    )(notes, rows, *extra)
    return (out[0][:, 0, :],) + tuple(out[1:])


def on_device(
    frontier,
    policy_table,
    first_counts,
    policy_index,
    owner_index,
    next_counts,
    value_in,
    value_out,
):
    devices = lax.axis_size("owner")
    mine = lax.axis_index("owner")
    capacity = RECV_DEV // devices
    kept_limit = NODE_DEV * devices
    line, chip, core = place_of(mine)
    lines, chips = devices // PLANE, PLANE // CORES
    first_root = ((core * chips + chip) * lines + line) * frontier.shape[0]
    onehots = [send_slots(owner_index[depth], devices, capacity) for depth in range(LEVELS)]
    slot_index = jnp.arange(SLOTS, dtype=jnp.int32)
    slots = [pick(onehot, slot_index + 1) - 1 for onehot in onehots]
    notes = list(slots)
    for depth in range(LEVELS):
        value = policy_index[depth]
        if depth < LEVELS - 1:
            value = value + HALF * next_counts[depth]
        notes.append(pick(onehots[depth], value))
    lineage = [first_root + jnp.arange(frontier.shape[0], dtype=jnp.int32)]
    counts = first_counts
    rows = frontier
    columns, root_columns, policy_rows = [], [], []
    for depth in range(LEVELS):
        parent, total = children_of(counts, slots[depth])
        notes += [pick(parent, part) for part in lineage]
        notes.append(jnp.broadcast_to(total, (devices, 1)))
        notes = jnp.concatenate(notes, axis=1)
        if depth == 0:
            received, rows = exchange(depth, notes, rows)
        else:
            wanted = jnp.stack(known, axis=1).astype(jnp.float32)
            received, rows, rows_known = exchange(depth, notes, rows, (wanted, policy_table.T))
            policy_rows.append(rows_known)
        if depth == 0:
            first = [
                received[:, k * capacity : (k + 1) * capacity] for k in range(2 * LEVELS)
            ]
            received = received[:, 2 * LEVELS * capacity :]
            known = [(part % HALF).reshape(-1) for part in first[LEVELS:]]
        lineage = [
            received[:, k * capacity : (k + 1) * capacity] for k in range(len(lineage))
        ]
        totals = received[:, len(lineage) * capacity]
        offsets = jnp.cumsum(totals) - totals
        slot = first[depth]
        policy = first[LEVELS + depth] % HALF
        kept = (slot >= 0) & (slot < totals[:, None]) & (offsets[:, None] + slot < kept_limit)
        if depth == 0:
            path = lineage + [policy]
        elif depth == 1:
            path = [lineage[0] % HALF, lineage[0] // HALF, policy]
        else:
            path = [lineage[0] % HALF, lineage[0] // HALF, lineage[1], policy]
        root_columns.append(jnp.where(kept, path[0], -1))
        columns += path[1:]
        counts = jnp.where(kept, first[LEVELS + depth] // HALF, 0).reshape(-1)
        path = [part.reshape(-1) for part in path]
        if depth > 0:
            known = path[1:2]
        lineage = [path[0] + HALF * path[1]] + path[2:]
        notes = []
    roots = rows.reshape(-1, rows.shape[-1])
    index = jnp.stack([part.reshape(-1) for part in columns + root_columns], axis=1)
    values = rebuild(
        index.astype(jnp.float32), *policy_rows, roots, policy_table.T, value_in, value_out.T
    )
    return jnp.swapaxes(values, 1, 2)


def solution(mesh):
    placed = (
        P("owner", None),
        P(),
        P("owner"),
        P(None, "owner"),
        P(None, "owner"),
        P(None, "owner"),
        P(),
        P(),
    )
    return jax.shard_map(
        on_device, mesh=mesh, in_specs=placed, out_specs=P(None, "owner", None), check_vma=False
    )
```

```python
import functools

import jax
import jax.numpy as jnp
from jax import lax
from jax.experimental import pallas as pl
from jax.experimental.pallas import tpu as pltpu
from jax.sharding import PartitionSpec as P

LEVELS = 3
SLOTS = 512
RECV_DEV = 512
NODE_DEV = 384
CORES = 2
PLANE = 8
HALF = 1 << 16
MESH = pl.DeviceIdType.MESH


def send_slots(owners, devices, capacity):
    slots = owners.shape[0]
    hit = owners[None, :] == jnp.arange(devices, dtype=jnp.int32)[:, None]
    upper = jnp.triu(jnp.ones((slots, slots), jnp.bfloat16))
    count = jnp.dot(hit.astype(jnp.bfloat16), upper, preferred_element_type=jnp.float32).astype(
        jnp.int32
    )
    rank = jnp.where(hit, count - 1, -1)
    return rank[:, None, :] == jnp.arange(capacity, dtype=jnp.int32)[None, :, None]


def pick(onehot, values):
    return jnp.sum(jnp.where(onehot, values[None, None, :], 0), axis=2)


def children_of(counts, slot):
    ends = jnp.cumsum(counts)
    parent = ((ends - counts)[None, None, :] <= slot[:, :, None]) & (
        slot[:, :, None] < ends[None, None, :]
    )
    return parent, jnp.minimum(ends[-1], SLOTS)


def step_place(step):
    level, begin = jnp.int32(0), jnp.int32(0)
    for depth in range(1, LEVELS):
        start = depth * (depth + 1) // 2
        level = jnp.where(step >= start, depth, level)
        begin = jnp.where(step >= start, start, begin)
    return level, step == begin, step == begin + level


def dot_last(left, right):
    return lax.dot_general(
        left, right, (((1,), (1,)), ((), ())), preferred_element_type=jnp.float32
    )


def column_of(index, place):
    lane = lax.broadcasted_iota(jnp.int32, index.shape, 1)
    return jnp.sum(jnp.where(lane == place, index, 0.0), axis=1, keepdims=True)


def picked(index, place, entries):
    entry = lax.broadcasted_iota(jnp.int32, (index.shape[0], entries), 1)
    onehot = jnp.where(entry.astype(jnp.float32) == column_of(index, place), 1.0, 0.0)
    return onehot.astype(jnp.bfloat16)


def rebuild_kernel(
    index_ref,
    policy_ref,
    second_ref,
    roots_hbm,
    table_hbm,
    in_hbm,
    out_hbm,
    values_ref,
    roots_ref,
    table_ref,
    in_ref,
    out_ref,
    rows_ref,
    factor_ref,
    sems,
):
    step = pl.program_id(0)
    level, first, last = step_place(step)
    copies = [
        pltpu.make_async_copy(source, target, sems.at[k])
        for k, (source, target) in enumerate(
            (
                (roots_hbm, roots_ref),
                (in_hbm, in_ref),
                (out_hbm, out_ref),
                (table_hbm, table_ref),
            )
        )
    ]

    @pl.when(step == 0)
    def _():
        for copy in copies:
            copy.start()
        copies[0].wait()

    @pl.when(step == 3)
    def _():
        copies[3].wait()

    index = index_ref[...]
    root_place = LEVELS * (LEVELS + 1) // 2 + level

    @pl.when(first)
    def _():
        rows_ref[...] = jnp.dot(
            picked(index, root_place, roots_ref.shape[0]),
            roots_ref[...],
            preferred_element_type=jnp.float32,
        ).astype(jnp.bfloat16)

    @pl.when(last)
    def _():
        factor_ref[...] = policy_ref[0]

    @pl.when(step == 1)
    def _():
        factor_ref[...] = second_ref[0]

    @pl.when(jnp.logical_not(last) & (step > 1))
    def _():
        factor = dot_last(picked(index, step, table_ref.shape[1]), table_ref[...])
        factor_ref[...] = factor.astype(jnp.bfloat16)

    rows = rows_ref[...].astype(jnp.float32) * factor_ref[...].astype(jnp.float32)
    mass = jnp.sum(rows, axis=1, keepdims=True)
    mass = jnp.where(column_of(index, root_place) >= 0.0, mass, 1.0)
    rows_ref[...] = (rows * (rows.shape[1] / mass)).astype(jnp.bfloat16)

    @pl.when(step == 0)
    def _():
        copies[1].wait()
        copies[2].wait()

    @pl.when(last)
    def _():
        hidden = jnp.dot(rows_ref[...], in_ref[...], preferred_element_type=jnp.float32)
        hidden = jnp.maximum(hidden, 0.0).astype(jnp.bfloat16)
        values_ref[0] = dot_last(out_ref[...], hidden).astype(jnp.bfloat16)


def rebuild(index, policy_rows, second_rows, roots, table, value_in, value_out):
    rows, hands = index.shape[0], table.shape[0]
    steps = LEVELS * (LEVELS + 1) // 2
    return pl.pallas_call(
        rebuild_kernel,
        grid=(steps,),
        out_shape=jax.ShapeDtypeStruct((LEVELS, hands, rows), jnp.bfloat16),
        in_specs=[
            pl.BlockSpec(index.shape, lambda step: (0, 0)),
            pl.BlockSpec((1, rows, hands), lambda step: (step_place(step)[0], 0, 0)),
            pl.BlockSpec((1, rows, hands), lambda step: (0, 0, 0)),
        ]
        + [pl.BlockSpec(memory_space=pl.ANY)] * 4,
        out_specs=pl.BlockSpec((1, hands, rows), lambda step: (step_place(step)[0], 0, 0)),
        scratch_shapes=[
            pltpu.VMEM(array.shape, array.dtype) for array in (roots, table, value_in, value_out)
        ]
        + [pltpu.VMEM((rows, hands), jnp.bfloat16)] * 2
        + [pltpu.SemaphoreType.DMA((4,))],
        compiler_params=pltpu.CompilerParams(vmem_limit_bytes=52 * 1024 * 1024),
    )(index, policy_rows, second_rows, roots, table, value_in, value_out)


def place_of(mine):
    return mine // PLANE, mine % PLANE // CORES, mine % CORES


def exchange_kernel(devices, stage, *refs):
    if len(refs) == 9:
        notes_ref, rows_ref, out_notes_ref, out_rows_ref = refs[:4]
    else:
        notes_ref, rows_ref, index_ref, table_hbm, out_notes_ref, out_rows_ref, policy_hbm = refs[:7]
        table_ref, policy_ref, policy_sem = refs[12:]
        refs = refs[3:12]
        load = pltpu.make_async_copy(table_hbm, table_ref, policy_sem.at[policy_ref.shape[0]])
        load.start()
    note_send, note_recv, row_send, row_recv, own_sem = refs[4:9]
    mine = lax.axis_index("owner")
    line, chip, core = place_of(mine)

    barrier = pltpu.get_barrier_semaphore()

    @pl.loop(1, devices)
    def _(turn):
        peer = lax.rem(mine + turn, devices)
        pl.semaphore_signal(barrier, inc=1, device_id=(peer,), device_id_type=MESH)

    pl.semaphore_wait(barrier, devices - 1)

    def note(turn):
        peer = lax.rem(mine + turn, devices)
        return pltpu.make_async_remote_copy(
            src_ref=notes_ref.at[peer],
            dst_ref=out_notes_ref.at[mine],
            send_sem=note_send.at[turn - 1],
            recv_sem=note_recv.at[turn - 1],
            device_id=(peer,),
            device_id_type=MESH,
        )

    @pl.loop(1, devices)
    def _(turn):
        note(turn).start()

    parts = out_rows_ref.shape[0]
    slot = (line, chip, core)[stage]
    moves = []
    for turn in range(1, parts):
        other = lax.rem(slot + turn, parts)
        peer = (
            other * PLANE + mine % PLANE,
            line * PLANE + other * CORES + core,
            line * PLANE + chip * CORES + other,
        )[stage]
        moves.append(
            pltpu.make_async_remote_copy(
                src_ref=rows_ref,
                dst_ref=out_rows_ref.at[slot],
                send_sem=row_send.at[turn - 1],
                recv_sem=row_recv.at[turn - 1],
                device_id=(peer,),
                device_id_type=MESH,
            )
        )
    for move in moves:
        move.start()
    own = (
        pltpu.make_async_copy(notes_ref.at[mine], out_notes_ref.at[mine], own_sem.at[0]),
        pltpu.make_async_copy(rows_ref, out_rows_ref.at[slot], own_sem.at[1]),
    )
    for copy in own:
        copy.start()

    if stage > 0:
        picks = policy_ref.shape[0]
        load.wait()

        def store(depth):
            return pltpu.make_async_copy(
                policy_ref.at[depth], policy_hbm.at[depth], policy_sem.at[depth]
            )

        @pl.loop(0, picks)
        def _(depth):
            onehot = picked(index_ref[...], depth, table_ref.shape[1])
            policy_ref[depth] = dot_last(onehot, table_ref[...]).astype(jnp.bfloat16)
            store(depth).start()

        for depth in range(picks):
            store(depth).wait()

    @pl.loop(1, devices)
    def _(turn):
        note(turn).wait()

    for move in moves:
        move.wait()
    for copy in own:
        copy.wait()


def exchange(stage, notes, rows, extra=()):
    devices = lax.axis_size("owner")
    parts = (devices // PLANE, PLANE // CORES, CORES)[stage]
    width = -(-notes.shape[1] // 128) * 128
    notes = jnp.pad(notes, ((0, 0), (0, width - notes.shape[1])))[:, None, :]
    vmem, anywhere = pl.BlockSpec(memory_space=pltpu.VMEM), pl.BlockSpec(memory_space=pl.ANY)
    out_shape = [
        jax.ShapeDtypeStruct(notes.shape, notes.dtype),
        jax.ShapeDtypeStruct((parts,) + rows.shape, rows.dtype),
    ]
    in_specs, out_specs = [vmem, vmem], [vmem, vmem]
    scratch = [
        pltpu.SemaphoreType.DMA((devices - 1,)),
        pltpu.SemaphoreType.DMA((devices - 1,)),
        pltpu.SemaphoreType.DMA((max(parts - 1, 1),)),
        pltpu.SemaphoreType.DMA((max(parts - 1, 1),)),
        pltpu.SemaphoreType.DMA((2,)),
    ]
    if extra:
        index, table = extra
        shape = (index.shape[1], index.shape[0], table.shape[0])
        out_shape.append(jax.ShapeDtypeStruct(shape, table.dtype))
        in_specs += [vmem, anywhere]
        out_specs.append(anywhere)
        scratch += [
            pltpu.VMEM(table.shape, table.dtype),
            pltpu.VMEM(shape, table.dtype),
            pltpu.SemaphoreType.DMA((index.shape[1] + 1,)),
        ]
    out = pl.pallas_call(
        functools.partial(exchange_kernel, devices, stage),
        out_shape=out_shape,
        in_specs=in_specs,
        out_specs=out_specs,
        scratch_shapes=scratch,
        compiler_params=pltpu.CompilerParams(
            collective_id=stage, has_side_effects=True, vmem_limit_bytes=48 * 1024 * 1024
        ),
    )(notes, rows, *extra)
    return (out[0][:, 0, :],) + tuple(out[1:])


def on_device(
    frontier,
    policy_table,
    first_counts,
    policy_index,
    owner_index,
    next_counts,
    value_in,
    value_out,
):
    devices = lax.axis_size("owner")
    mine = lax.axis_index("owner")
    capacity = RECV_DEV // devices
    kept_limit = NODE_DEV * devices
    line, chip, core = place_of(mine)
    lines, chips = devices // PLANE, PLANE // CORES
    first_root = ((core * chips + chip) * lines + line) * frontier.shape[0]
    onehots = [send_slots(owner_index[depth], devices, capacity) for depth in range(LEVELS)]
    slot_index = jnp.arange(SLOTS, dtype=jnp.int32)
    slots = [pick(onehot, slot_index + 1) - 1 for onehot in onehots]
    notes = list(slots)
    for depth in range(LEVELS):
        value = policy_index[depth]
        if depth < LEVELS - 1:
            value = value + HALF * next_counts[depth]
        notes.append(pick(onehots[depth], value))
    lineage = [first_root + jnp.arange(frontier.shape[0], dtype=jnp.int32)]
    counts = first_counts
    rows = frontier
    columns, root_columns, policy_rows = [], [], []
    for depth in range(LEVELS):
        parent, total = children_of(counts, slots[depth])
        notes += [pick(parent, part) for part in lineage]
        notes.append(jnp.broadcast_to(total, (devices, 1)))
        notes = jnp.concatenate(notes, axis=1)
        if depth == 0:
            received, rows = exchange(depth, notes, rows)
        else:
            wanted = jnp.stack(known, axis=1).astype(jnp.float32)
            received, rows, rows_known = exchange(depth, notes, rows, (wanted, policy_table.T))
            policy_rows.append(rows_known)
        if depth == 0:
            first = [
                received[:, k * capacity : (k + 1) * capacity] for k in range(2 * LEVELS)
            ]
            received = received[:, 2 * LEVELS * capacity :]
            known = [(part % HALF).reshape(-1) for part in first[LEVELS:]]
        lineage = [
            received[:, k * capacity : (k + 1) * capacity] for k in range(len(lineage))
        ]
        totals = received[:, len(lineage) * capacity]
        offsets = jnp.cumsum(totals) - totals
        slot = first[depth]
        policy = first[LEVELS + depth] % HALF
        kept = (slot >= 0) & (slot < totals[:, None]) & (offsets[:, None] + slot < kept_limit)
        if depth == 0:
            path = lineage + [policy]
        elif depth == 1:
            path = [lineage[0] % HALF, lineage[0] // HALF, policy]
        else:
            path = [lineage[0] % HALF, lineage[0] // HALF, lineage[1], policy]
        root_columns.append(jnp.where(kept, path[0], -1))
        columns += path[1:]
        counts = jnp.where(kept, first[LEVELS + depth] // HALF, 0).reshape(-1)
        path = [part.reshape(-1) for part in path]
        if depth > 0:
            known = path[1:2]
        lineage = [path[0] + HALF * path[1]] + path[2:]
        notes = []
    roots = rows.reshape(-1, rows.shape[-1])
    index = jnp.stack([part.reshape(-1) for part in columns + root_columns], axis=1)
    values = rebuild(
        index.astype(jnp.float32), *policy_rows, roots, policy_table.T, value_in, value_out.T
    )
    return jnp.swapaxes(values, 1, 2)


def solution(mesh):
    placed = (
        P("owner", None),
        P(),
        P("owner"),
        P(None, "owner"),
        P(None, "owner"),
        P(None, "owner"),
        P(),
        P(),
    )
    return jax.shard_map(
        on_device, mesh=mesh, in_specs=placed, out_specs=P(None, "owner", None), check_vma=False
    )
```
